32 devices in a mesh: row: 4 (over y, x), col: 8 (over z, core).
Axes of the slice: x: 2, y: 2, z: 4, core: 2. Of those that a mesh axis runs over, the one named last changes fastest.
Arguments:
- inputs: bfloat16 [1024, 8192], P('col', 'row'), may hold values from -6 to 6
- gate_weight: bfloat16 [8192, 14336], P('row', 'col'), may hold values from -0.125 to 0.125
- up_weight: bfloat16 [8192, 14336], P('row', 'col'), may hold values from -0.125 to 0.125
- down_weight: bfloat16 [14336, 8192], P('col', 'row'), may hold values from -0.09375 to 0.09375
- gate_mask: int32 [64, 112], P('row', 'col'), may hold values 0 or 1
- up_mask: int32 [64, 112], P('row', 'col'), may hold values 0 or 1
- down_mask: int32 [112, 64], P('col', 'row'), may hold values 0 or 1
- cotangent: bfloat16 [1024, 8192], P('col', 'row'), may hold values from -6 to 6
Outputs:
- outputs: bfloat16 [1024, 8192], P('col', 'row')
- input_grad: bfloat16 [1024, 8192], P('col', 'row')
- gate_grad: bfloat16 [8192, 14336], P('row', 'col')
- up_grad: bfloat16 [8192, 14336], P('row', 'col')
- down_grad: bfloat16 [14336, 8192], P('col', 'row')
The draws below stay inside these ranges and needn't reach their ends.
All inputs are finite; a program needn't handle non-finite values. No bound on the sum of `gate_mask` or of `up_mask` or of `down_mask` on one device may be relied on, other than what follows from the above.
Results may differ from the reference program's by a relative error of at most 0.005.
Values may be sent and summed in bfloat16 or wider, within the bound.
A program may use at most 192 MiB of HBM per device.

```python
import jax
import jax.numpy as jnp

D = 8192
FF = 14336
BLOCK = 128
TOKENS = 1024


def with_ends(values, rng, low, high):
    spot = [jax.random.randint(jax.random.fold_in(rng, axis), (), 0, length) for axis, length in enumerate(values.shape)]
    widest = values.shape.index(max(values.shape))
    neighbour = spot[:widest] + [(spot[widest] + 1) % values.shape[widest]] + spot[widest + 1:]
    return values.at[tuple(spot)].set(low).at[tuple(neighbour)].set(high)


def steps_of(key, shape, split, least, top_value):
    factor_of, own = 1.0, jax.random.fold_in(key, 6)
    for position, shards_of in split:
        draws = jnp.exp(jax.random.uniform(jax.random.fold_in(own, position), (shards_of,), jnp.float32, least / len(split), top_value / len(split)))
        factor_of = factor_of * jnp.repeat(draws, shape[position] // shards_of).reshape([-1 if axis == position else 1 for axis in range(len(shape))])
    return factor_of


def noise(rng, dims, deviation, most, pieces=(), held_as=jnp.bfloat16):
    drawn = jax.random.normal(rng, dims, jnp.float32) * deviation
    if len(pieces) > 0:
        drawn = steps_of(rng, dims, pieces, -0.22, 0.18) * drawn
    return jnp.clip(drawn, min=-most, max=most).astype(held_as)


def setup_inputs(seed: int = 0) -> dict:
    seeds = jax.random.split(jax.random.key(seed), 9)
    return {
        "inputs": noise(seeds[0], (TOKENS, D), 1.0, 6.0, ((0, 8), (1, 4))),
        "gate_weight": noise(seeds[1], (D, FF), (D // 4) ** -0.5, 0.125, ((0, 4), (1, 8))),
        "up_weight": noise(seeds[2], (D, FF), (D // 4) ** -0.5, 0.125, ((0, 4), (1, 8))),
        "down_weight": noise(seeds[3], (FF, D), (FF // 4) ** -0.5, 0.09375, ((0, 8), (1, 4))),
        "gate_mask": with_ends((jax.random.randint(seeds[4], (D // BLOCK, FF // BLOCK), 0, 4) < 1).astype(jnp.int32), jax.random.fold_in(seeds[4], 1), 0, 1),
        "up_mask": with_ends((jax.random.randint(seeds[5], (D // BLOCK, FF // BLOCK), 0, 4) < 1).astype(jnp.int32), jax.random.fold_in(seeds[5], 1), 0, 1),
        "down_mask": with_ends((jax.random.randint(seeds[6], (FF // BLOCK, D // BLOCK), 0, 4) < 1).astype(jnp.int32), jax.random.fold_in(seeds[6], 1), 0, 1),
        "cotangent": noise(seeds[7], (TOKENS, D), 1.0, 6.0, ((0, 8), (1, 4))),
    }


def apply_mask(weights, mask):
    blocks_r, blocks_c = mask.shape
    rows, cols = weights.shape
    shaped = weights.reshape(blocks_r, rows // blocks_r, blocks_c, cols // blocks_c)
    shaped = shaped * mask[:, None, :, None].astype(weights.dtype)
    return shaped.reshape(rows, cols)


def reference(inputs, gate_weight, up_weight, down_weight, gate_mask, up_mask, down_mask, cotangent):
    gate_masked = apply_mask(gate_weight, gate_mask)
    up_masked = apply_mask(up_weight, up_mask)
    down_masked = apply_mask(down_weight, down_mask)
    gate = jnp.dot(inputs, gate_masked, preferred_element_type=jnp.float32)
    up = jnp.dot(inputs, up_masked, preferred_element_type=jnp.float32)
    sig = jax.nn.sigmoid(gate)
    hidden = (gate * sig * up).astype(jnp.bfloat16)
    outputs = jnp.dot(hidden, down_masked, preferred_element_type=jnp.float32).astype(jnp.bfloat16)
    hidden_cot = jnp.dot(cotangent, down_masked.T, preferred_element_type=jnp.float32)
    gate_cot = (hidden_cot * up * sig * (1.0 + gate * (1.0 - sig))).astype(jnp.bfloat16)
    up_cot = (hidden_cot * gate * sig).astype(jnp.bfloat16)
    down_grad = jnp.dot(hidden.T, cotangent, preferred_element_type=jnp.float32).astype(jnp.bfloat16)
    gate_grad = jnp.dot(inputs.T, gate_cot, preferred_element_type=jnp.float32).astype(jnp.bfloat16)
    up_grad = jnp.dot(inputs.T, up_cot, preferred_element_type=jnp.float32).astype(jnp.bfloat16)
    input_grad = (jnp.dot(gate_cot, gate_masked.T, preferred_element_type=jnp.float32)
                  + jnp.dot(up_cot, up_masked.T, preferred_element_type=jnp.float32)).astype(jnp.bfloat16)
    return outputs, input_grad, gate_grad, up_grad, down_grad
```

```python
import functools

import jax
import jax.numpy as jnp
from jax import lax
from jax.sharding import PartitionSpec as P


def apply_mask(weights, mask):
    blocks_r, blocks_c = mask.shape
    rows, cols = weights.shape
    shaped = weights.reshape(blocks_r, rows // blocks_r, blocks_c, cols // blocks_c)
    shaped = shaped * mask[:, None, :, None].astype(weights.dtype)
    return shaped.reshape(rows, cols)


def contract_rows(left, right):
    return lax.dot_general(
        left, right, (((0,), (0,)), ((), ())), preferred_element_type=jnp.float32
    )


def contract_cols(left, right):
    return lax.dot_general(
        left, right, (((1,), (1,)), ((), ())), preferred_element_type=jnp.float32
    )


def swap(value, bit, count):
    return lax.ppermute(value, "row", [(r, r ^ bit) for r in range(count)])


def side(value, bit, mine):
    count = value.shape[0]
    split = value.reshape(count // (2 * bit), 2, bit, *value.shape[1:])
    return lax.dynamic_index_in_dim(split, mine, 1, keepdims=False).reshape(count // 2, *value.shape[1:])


def scatter_begin(left, right, dot, order, count):
    me = lax.axis_index("row")
    blocks = left.reshape(count, -1, left.shape[1])
    first = order[0]
    away = side(blocks, first, 1 - (me // first) % 2).reshape(-1, left.shape[1])
    return swap(dot(away, right).astype(jnp.bfloat16), first, count)


def scatter_finish(got, left, right, dot, order, count):
    me = lax.axis_index("row")
    blocks = left.reshape(count, -1, left.shape[1])
    first, second = order
    at_second = (me // second) % 2
    stay = side(blocks, first, (me // first) % 2)
    relay = lax.dynamic_index_in_dim(stay, 1 - at_second, 0, keepdims=False)
    own = lax.dynamic_index_in_dim(stay, at_second, 0, keepdims=False)
    got = got.reshape(2, -1, got.shape[1])
    relayed = dot(relay, right) + lax.dynamic_index_in_dim(got, 1 - at_second, 0, keepdims=False).astype(jnp.float32)
    last = swap(relayed.astype(jnp.bfloat16), second, count)
    kept = dot(own, right) + lax.dynamic_index_in_dim(got, at_second, 0, keepdims=False).astype(jnp.float32)
    return kept + last.astype(jnp.float32)


def scatter_plain(left, right, dot):
    part = dot(left, right).astype(jnp.bfloat16)
    return lax.psum_scatter(part, "row", scatter_dimension=0, tiled=True).astype(jnp.float32)


def gather_begin(value, order, count):
    return swap(value, order[0], count), swap(value, order[1], count)


def gather_finish(value, hops, order, count):
    me = lax.axis_index("row")
    first, second = order
    near, far = hops
    corner = swap(near, second, count)
    rows, cols = value.shape
    full = jnp.zeros((count * rows, cols), value.dtype)
    for piece, owner in ((value, me), (near, me ^ first), (far, me ^ second), (corner, me ^ (first | second))):
        full = lax.dynamic_update_slice(full, piece, (owner * rows, 0))
    return full


def gather_plain(value):
    return lax.all_gather(value, "row", axis=0, tiled=True)


def col_plain(value):
    return lax.psum_scatter(value, "col", scatter_dimension=0, tiled=True).astype(jnp.bfloat16)


def col_direct(value, count):
    me = lax.axis_index("col")
    chips = count // 2
    core, z = me % 2, me // 2
    blocks = value.reshape(chips, 2, -1, value.shape[1])
    give = lax.dynamic_index_in_dim(blocks, 1 - core, 1, keepdims=False)
    keep = lax.dynamic_index_in_dim(blocks, core, 1, keepdims=False)
    both = keep + lax.ppermute(give, "col", [(c, c ^ 1) for c in range(count)])
    total = lax.dynamic_index_in_dim(both, z, 0, keepdims=False)
    for step in range(1, chips):
        piece = lax.dynamic_index_in_dim(both, z ^ step, 0, keepdims=False).astype(jnp.bfloat16)
        total = total + lax.ppermute(piece, "col", [(c, c ^ (2 * step)) for c in range(count)]).astype(jnp.float32)
    return total.astype(jnp.bfloat16)


def weight_grads(inputs_all, cot_all, hidden_all, gate_cot_all, up_cot_all):
    down_grad = contract_rows(hidden_all, cot_all).astype(jnp.bfloat16)
    gate_grad = contract_rows(inputs_all, gate_cot_all).astype(jnp.bfloat16)
    up_grad = contract_rows(inputs_all, up_cot_all).astype(jnp.bfloat16)
    return gate_grad, up_grad, down_grad


def plain(left, right):
    return jnp.dot(left, right, preferred_element_type=jnp.float32)


def swiglu(gate, up, hidden_cot):
    sig = jax.nn.sigmoid(gate)
    hidden = (gate * sig * up).astype(jnp.bfloat16)
    gate_cot = (hidden_cot * up * sig * (1.0 + gate * (1.0 - sig))).astype(jnp.bfloat16)
    up_cot = (hidden_cot * gate * sig).astype(jnp.bfloat16)
    return hidden, gate_cot, up_cot


def body(count, cols, inputs, gate_weight, up_weight, down_weight, gate_mask, up_mask, down_mask, cotangent):
    cot_all = lax.all_gather(cotangent, "col", axis=0, tiled=True)
    inputs_all = lax.all_gather(inputs, "col", axis=0, tiled=True)
    gate_masked = apply_mask(gate_weight, gate_mask)
    up_masked = apply_mask(up_weight, up_mask)
    down_masked = apply_mask(down_weight, down_mask)
    half = gate_masked.shape[1] // 2
    if count != 4 or cols != 8:
        gate = scatter_plain(inputs_all, gate_masked, plain)
        up = scatter_plain(inputs_all, up_masked, plain)
        hidden, gate_cot, up_cot = swiglu(gate, up, scatter_plain(cot_all, down_masked, contract_cols))
        hidden_all, gate_cot_all, up_cot_all = gather_plain(hidden), gather_plain(gate_cot), gather_plain(up_cot)
        outputs = col_plain(plain(hidden_all, down_masked))
        input_grad = col_plain(contract_cols(gate_cot_all, gate_masked) + contract_cols(up_cot_all, up_masked))
        return (outputs, input_grad, *weight_grads(inputs_all, cot_all, hidden_all, gate_cot_all, up_cot_all))
    A, B = (1, 2), (2, 1)
    low, high = down_masked[:half], down_masked[half:]
    got_low = scatter_begin(cot_all, low, contract_cols, A, count)
    got_high = scatter_begin(cot_all, high, contract_cols, B, count)
    inputs_all, got_low, got_high = lax.optimization_barrier((inputs_all, got_low, got_high))
    got_gate = scatter_begin(inputs_all, gate_masked, plain, A, count)
    got_up = scatter_begin(inputs_all, up_masked, plain, B, count)
    hidden_cot = jnp.concatenate(
        [
            scatter_finish(got_low, cot_all, low, contract_cols, A, count),
            scatter_finish(got_high, cot_all, high, contract_cols, B, count),
        ],
        axis=1,
    )
    gate = scatter_finish(got_gate, inputs_all, gate_masked, plain, A, count)
    up = scatter_finish(got_up, inputs_all, up_masked, plain, B, count)
    hidden, gate_cot, up_cot = swiglu(gate, up, hidden_cot)
    hidden_low, hidden_high = hidden[:, :half], hidden[:, half:]
    hops_low, hops_high = gather_begin(hidden_low, A, count), gather_begin(hidden_high, B, count)
    hops_gate, hops_up = gather_begin(gate_cot, A, count), gather_begin(up_cot, B, count)
    hidden_all = jnp.concatenate(
        [gather_finish(hidden_low, hops_low, A, count), gather_finish(hidden_high, hops_high, B, count)], axis=1
    )
    hidden_all, hops_gate, hops_up = lax.optimization_barrier((hidden_all, hops_gate, hops_up))
    outputs = col_plain(plain(hidden_all, down_masked))
    gate_cot_all = gather_finish(gate_cot, hops_gate, A, count)
    up_cot_all = gather_finish(up_cot, hops_up, B, count)
    input_grad = col_direct(contract_cols(gate_cot_all, gate_masked) + contract_cols(up_cot_all, up_masked), cols)
    return (outputs, input_grad, *weight_grads(inputs_all, cot_all, hidden_all, gate_cot_all, up_cot_all))


def solution(mesh):
    return jax.shard_map(
        functools.partial(body, mesh.shape["row"], mesh.shape["col"]),
        mesh=mesh,
        in_specs=(
            P("col", "row"),
            P("row", "col"),
            P("row", "col"),
            P("col", "row"),
            P("row", "col"),
            P("row", "col"),
            P("col", "row"),
            P("col", "row"),
        ),
        out_specs=(
            P("col", "row"),
            P("col", "row"),
            P("row", "col"),
            P("row", "col"),
            P("col", "row"),
        ),
        check_vma=False,
    )
```
